32 devices in a mesh: ens: 2 (over x), row: 16 (over z, y, core).
Axes of the slice: x: 2, y: 2, z: 4, core: 2. Of those that a mesh axis runs over, the one named last changes fastest.
Arguments:
- l_panel: float32 [2048, 24576], P('ens', 'row'), parts along dimension 0, may hold values from -0.0546875 to 0.0546875
- x_prior: float32 [24576, 2048], P('row', 'ens'), parts along dimension 1, may hold values from -6 to 6
- b_rows: float32 [1024, 2048], P('row', 'ens'), parts along dimension 1, may hold values from -6 to 6
- diag_blocks: float32 [4, 512, 512], P('ens'), parts along dimension 0, as said below
- coupling: float32 [1024, 512], P('ens'), parts along dimension 0, may hold values from -0.25 to 0.25
Outputs:
- solved: float32 [1024, 2048], P('row', 'ens'), parts along dimension 1
The draws below stay inside these ranges and needn't reach their ends.
There are 2 independent parts, one for each index of `ens`. The reference program is written for one: setup_inputs(seed, part) draws one part's arguments, and reference() takes and returns one part's arrays. A program takes and returns all parts, laid end to end along the dimension named above; each array names one. Nothing has to cross between parts.
Inputs may be any that keep to these rules, and one draw needn't show every extreme that they name: `diag_blocks`: lower triangular; diagonal entries between 1.5 and 3.
All inputs are finite; a program needn't handle non-finite values.
Results may differ from the reference program's by a relative error of at most 0.00007.
Values sent between devices are 32-bit elements; how exact they have to be, the bound alone decides.
A program may use at most 64 MiB of HBM per device.

```python
import math
import jax
import jax.numpy as jnp
from jax import lax

BLOCK = 512
NRHS = 1024
PRIOR = 24576
ROWS = 1024


def draw_diag_blocks(key, part):
    key_off = jax.random.fold_in(key, 11)
    key_diag = jax.random.fold_in(key, 23)
    offdiag = jax.random.normal(key_off, (2, BLOCK, BLOCK), jnp.float32)
    offdiag = offdiag / math.sqrt(BLOCK)
    diagonal = jax.random.uniform(key_diag, (2, BLOCK), jnp.float32, 1.5, 3.0)
    row_ids = lax.broadcasted_iota(jnp.int32, (BLOCK, BLOCK), 0)
    col_ids = lax.broadcasted_iota(jnp.int32, (BLOCK, BLOCK), 1)
    lower_part = jnp.where(row_ids > col_ids, offdiag, 0.0)
    return lower_part + jnp.where(row_ids == col_ids, diagonal[:, :, None], 0.0)


def raised(result, own_key, source, target, parts, factor):
    def block_of(position):
        return (jnp.arange(result.shape[position]) // (result.shape[position] // parts)).reshape((-1,) + (1,) * (result.ndim - 1 - position))

    first = jax.random.permutation(own_key, parts)[block_of(target)]
    far = (block_of(target) + parts // 2) % parts
    return jnp.where((block_of(source) == first) | (block_of(source) == far), factor * result, result)


def level_of(key, shape, pieces, low, high):
    def one(dim, parts):
        draws = jax.random.uniform(jax.random.fold_in(jax.random.fold_in(key, 6), dim), (parts,), jnp.float32, low / len(pieces), high / len(pieces))
        return jnp.repeat(jnp.exp(draws), shape[dim] // parts).reshape((-1,) + (1,) * (len(shape) - dim - 1))

    loudness = one(*pieces[0])
    for cut in pieces[1:]:
        loudness = loudness * one(*cut)
    return loudness


def normal_values(own_key, extent, spread, limit, pieces=(), dtype=jnp.bfloat16):
    gain = level_of(own_key, extent, pieces, -0.22, 0.18) if pieces else 1.0
    result = jax.random.normal(own_key, extent, jnp.float32) * spread * gain
    return jnp.minimum(jnp.maximum(result, -limit), limit).astype(dtype)


def bell_draw_with(own_key, dims, spread, bound, shards, heavy, held_as=jnp.bfloat16):
    entries = spread * jax.random.normal(own_key, dims, jnp.float32)
    if shards:
        entries = entries * level_of(own_key, dims, shards, -0.22, 0.18)
    return jnp.clip(raised(entries, jax.random.fold_in(own_key, 3), *heavy), -bound, bound).astype(held_as)


def setup_inputs(seed: int = 0, part: int = 0) -> dict:
    key_list = jax.random.split(jax.random.key(seed), 6)
    own_keys = jax.random.split(jax.random.fold_in(key_list[5], part), 6)
    l_panel = bell_draw_with(own_keys[0], (ROWS, PRIOR), PRIOR ** -0.5, 0.0546875, ((1, 16),), (1, 0, 16, 2.0), jnp.float32)
    x_prior = normal_values(own_keys[1], (PRIOR, NRHS), 1.0, 6.0, ((0, 16),), jnp.float32)
    b_rows = normal_values(own_keys[2], (ROWS, NRHS), 1.0, 6.0, ((0, 16),), jnp.float32)
    diag_blocks = draw_diag_blocks(jax.random.fold_in(jax.random.fold_in(key_list[5], part), 71), part)
    coupling = normal_values(own_keys[4], (BLOCK, BLOCK), BLOCK ** -0.5, 0.25, (), jnp.float32)
    return {"l_panel": l_panel, "x_prior": x_prior, "b_rows": b_rows, "diag_blocks": diag_blocks, "coupling": coupling}


def lower_solve(matrix, rhs):
    return lax.linalg.triangular_solve(matrix, rhs, left_side=True, lower=True)

def reference(l_panel, x_prior, b_rows, diag_blocks, coupling):
    update = jnp.dot(l_panel.astype(jnp.float32), x_prior.astype(jnp.float32), precision=lax.Precision.HIGHEST, preferred_element_type=jnp.float32)
    residual = b_rows - update
    block_rows = diag_blocks.shape[1]
    first_part = lower_solve(diag_blocks[0], residual[:block_rows])
    second_rhs = residual[block_rows:] - jnp.dot(coupling.astype(jnp.float32), first_part.astype(jnp.float32), precision=lax.Precision.HIGHEST, preferred_element_type=jnp.float32)
    second_part = lower_solve(diag_blocks[1], second_rhs)
    return jnp.concatenate([first_part, second_part], axis=0)
```

```python
import functools

import jax
import jax.numpy as jnp
from jax import lax
from jax.experimental import pallas as pl
from jax.experimental.pallas import tpu as pltpu
from jax.sharding import PartitionSpec as P

MESH = pl.DeviceIdType.MESH
F32, BF16 = jnp.float32, jnp.bfloat16


def split(value):
    high = value.astype(BF16)
    return high, (value - high.astype(F32)).astype(BF16)


def mm(a, b):
    return jnp.dot(a, b, preferred_element_type=F32)


def dot3(a, b):
    return mm(a[0], b[0]) + mm(a[0], b[1]) + mm(a[1], b[0])


def inverses(blocks):
    size = blocks[0].shape[0]
    rows = lax.broadcasted_iota(jnp.int32, (size, size), 0)
    cols = lax.broadcasted_iota(jnp.int32, (size, size), 1)
    on_diag = rows == cols
    eye = jnp.where(on_diag, 1.0, 0.0)
    scaled, col_scale = [], []
    for block in blocks:
        diag = jnp.where(on_diag, block, 0.0)
        scaled.append(block / jnp.sum(diag, axis=1, keepdims=True))
        col_scale.append(1.0 / jnp.sum(diag, axis=0, keepdims=True))
    step = 8
    near = (rows > cols) & (rows // step == cols // step)
    low = [jnp.where(near, s, 0.0) for s in scaled]
    ls = [split(v) for v in low]
    sq = [dot3(v, v) for v in ls]
    sqs = [split(v) for v in sq]
    quad = [dot3(v, v) for v in sqs]
    inv = [eye - v for v in low]
    inv = [v + dot3(split(v), w) for v, w in zip(inv, sqs)]
    inv = [v + dot3(split(v), split(w)) for v, w in zip(inv, quad)]
    while step < size:
        wide = 2 * step
        below = (rows // wide == cols // wide) & (rows // step > cols // step)
        invs = [split(v) for v in inv]
        prod = [dot3(split(jnp.where(below, s, 0.0)), v) for s, v in zip(scaled, invs)]
        inv = [v - dot3(w, split(p)) for v, w, p in zip(inv, invs, prod)]
        step = wide
    return [v * c for v, c in zip(inv, col_scale)]


def kernel(n, l_hbm, x_hbm, b_hbm, d_hbm, c_hbm, out_ref,
           l32, x32, b32, d32, c32, lhi, llo, xhi, xlo, fhi, flo, ihi, ilo, pbuf, shi, slo,
           sbuf, prcv, yrcv, urcv, drcv,
           in_sem, l_sem, x_sem, psend, precv, ysend, yrecv, usend, urecv, dsend, drecv):
    me = lax.axis_index("row")
    core, y, z = me % 2, (me // 2) % 2, me // 4
    depth = n // 4
    tiles, _, _, _, own, width = sbuf.shape
    rows = l32.shape[0]
    half = d32.shape[1]
    piece = ihi.shape[1]
    parts = rows // piece
    partner = me + 1 - 2 * core
    across = me + 2 - 4 * y
    up, down = me + 4, me - 4

    def send(src, dst, ssem, rsem, target):
        return pltpu.make_async_remote_copy(
            src_ref=src, dst_ref=dst, send_sem=ssem, recv_sem=rsem,
            device_id={"row": target}, device_id_type=MESH)

    def local(src, dst, sem):
        return pltpu.make_async_copy(src, dst, sem)

    in_copies = [local(d_hbm, d32, in_sem.at[0]), local(c_hbm, c32, in_sem.at[1]),
                 local(b_hbm, b32, in_sem.at[2])]
    l_copies = [local(l_hbm.at[pl.ds(k * piece, piece)], l32.at[pl.ds(k * piece, piece)], l_sem.at[k])
                for k in range(parts)]

    def x_copy(t):
        cols = pl.ds(pl.multiple_of(t * width, width), width)
        return local(x_hbm.at[:, cols], x32.at[t], x_sem.at[t])

    in_copies[0].start()
    x_copy(0).start()
    for copy in l_copies:
        copy.start()
    in_copies[1].start()
    in_copies[2].start()
    for t in range(1, tiles):
        x_copy(t).start()

    barrier = pltpu.get_barrier_semaphore()

    def greet(target):
        pl.semaphore_signal(barrier, inc=1, device_id={"row": target}, device_id_type=MESH)

    greet(partner)
    greet(across)

    @pl.when(z > 0)
    def _():
        greet(down)

    @pl.when(z < depth - 1)
    def _():
        greet(up)

    in_copies[0].wait()
    blocks = []
    for k in range(parts):
        which, at = (k * piece) // half, (k * piece) % half
        blocks.append(d32[which, at:at + piece, at:at + piece])
    for k, inv in enumerate(inverses(blocks)):
        ihi[k], ilo[k] = split(inv)
    for which in range(2):
        r = slice(which * half, (which + 1) * half)
        fhi[r, r], flo[r, r] = split(d32[which])
    in_copies[1].wait()
    fhi[half:, :half], flo[half:, :half] = split(c32[...])
    for k in range(parts):
        l_copies[k].wait()
        r = slice(k * piece, (k + 1) * piece)
        lhi[r], llo[r] = split(l32[r])
    in_copies[2].wait()

    inside = (z > 0).astype(jnp.int32) + (z < depth - 1).astype(jnp.int32)
    pl.semaphore_wait(barrier, 2 + inside)

    def pair_copy(t):
        return send(sbuf.at[t, 1 - core], prcv.at[t], psend.at[t], precv.at[t], partner)

    def y_copy(t):
        return send(sbuf.at[t, core, 1 - y], yrcv.at[t], ysend.at[t], yrecv.at[t], across)

    def up_copy(t, o):
        return send(sbuf.at[t, core, y, o], urcv.at[t, o], usend.at[t, o], urecv.at[t, o], up)

    def down_copy(t, o):
        return send(sbuf.at[t, core, y, o], drcv.at[t, o], dsend.at[t, o], drecv.at[t, o], down)

    def stage_y(t):
        pair_copy(t).wait_recv()
        sbuf[t, core, 1 - y] += prcv[t, 1 - y]
        y_copy(t).start()
        sbuf[t, core, y] += prcv[t, y]

    def stage_z(t):
        y_copy(t).wait_recv()
        sbuf[t, core, y] += yrcv[t]

        @pl.when(z == 0)
        def _():
            for o in range(depth - 1, 0, -1):
                up_copy(t, o).start()

        @pl.when(z == depth - 1)
        def _():
            for o in range(depth - 1):
                down_copy(t, o).start()

    def ups(t):
        for o in range(depth - 1, 1, -1):
            @pl.when((z > 0) & (z < o))
            def _():
                up_copy(t, o).wait_recv()
                sbuf[t, core, y, o] += urcv[t, o]
                up_copy(t, o).start()

    def downs(t):
        for o in range(depth - 2):
            @pl.when((z < depth - 1) & (z > o))
            def _():
                down_copy(t, o).wait_recv()
                sbuf[t, core, y, o] += drcv[t, o]
                down_copy(t, o).start()

    def relay(t):
        lower = z < depth // 2

        @pl.when(lower)
        def _():
            ups(t)
            downs(t)

        @pl.when(jnp.logical_not(lower))
        def _():
            downs(t)
            ups(t)

        @pl.when(z > 0)
        def _():
            up_copy(t, z).wait_recv()
            sbuf[t, core, y, z] += urcv[t, z]

        @pl.when(z < depth - 1)
        def _():
            down_copy(t, z).wait_recv()
            sbuf[t, core, y, z] += drcv[t, z]

        cols = pl.ds(pl.multiple_of(t * width, width), width)
        out_ref[:, cols] = -sbuf[t, core, y, z]

    def product(first, last):
        def step(k, carry):
            r = pl.ds(pl.multiple_of(k * piece, piece), piece)
            pbuf[r, :] = dot3((lhi[r, :], llo[r, :]), (xhi[...], xlo[...]))
            return carry
        lax.fori_loop(first, last, step, 0)

    def tile(t, carry):
        x_copy(t).wait()
        xhi[...], xlo[...] = split(x32[t])
        product(0, parts // 2)

        @pl.when(t >= 1)
        def _():
            stage_y(t - 1)

        product(parts // 2, parts)

        @pl.when(t >= 2)
        def _():
            stage_z(t - 2)

        mine = pl.ds(pl.multiple_of(me * own, own), own)
        cols = pl.ds(pl.multiple_of(t * width, width), width)
        pbuf[mine, :] -= b32[:, cols]
        for k in range(parts):
            r = slice(k * piece, (k + 1) * piece)
            rest = pbuf[r, :]
            if k:
                done = slice(0, k * piece)
                rest = rest - dot3((fhi[r, done], flo[r, done]), (shi[done, :], slo[done, :]))
            value = dot3((ihi[k], ilo[k]), split(rest))
            shi[r, :], slo[r, :] = split(value)
            for p in range(piece // own):
                g = k * (piece // own) + p
                sbuf[t, g % 2, (g // 2) % 2, g // 4] = value[p * own:(p + 1) * own]
        pair_copy(t).start()

        @pl.when(t >= 2)
        def _():
            relay(t - 2)

        return carry

    lax.fori_loop(0, tiles, tile, 0)
    stage_y(tiles - 1)
    if tiles > 1:
        stage_z(tiles - 2)
        relay(tiles - 2)
    stage_z(tiles - 1)
    relay(tiles - 1)

    def finish(t, carry):
        pair_copy(t).wait_send()
        y_copy(t).wait_send()
        for o in range(depth):
            @pl.when(z < o)
            def _():
                up_copy(t, o).wait_send()

            @pl.when(z > o)
            def _():
                down_copy(t, o).wait_send()
        return carry

    lax.fori_loop(0, tiles, finish, 0)


def shards(n, l_panel, x_prior, b_rows, diag_blocks, coupling):
    rows, inner = l_panel.shape
    nrhs = x_prior.shape[1]
    own = b_rows.shape[0]
    half = diag_blocks.shape[1]
    width = min(nrhs, 256)
    piece = min(half, 256)
    tiles, depth, parts = nrhs // width, n // 4, rows // piece
    dma = pltpu.SemaphoreType.DMA
    vmem = pltpu.VMEM
    any_spec = pl.BlockSpec(memory_space=pl.ANY)
    return pl.pallas_call(
        functools.partial(kernel, n),
        out_shape=jax.ShapeDtypeStruct((own, nrhs), F32),
        in_specs=[any_spec] * 5,
        out_specs=pl.BlockSpec(memory_space=pltpu.VMEM),
        scratch_shapes=[
            vmem((rows, inner), F32), vmem((tiles, inner, width), F32), vmem((own, nrhs), F32),
            vmem(diag_blocks.shape, F32), vmem(coupling.shape, F32),
            vmem((rows, inner), BF16), vmem((rows, inner), BF16),
            vmem((inner, width), BF16), vmem((inner, width), BF16),
            vmem((rows, rows), BF16), vmem((rows, rows), BF16),
            vmem((parts, piece, piece), BF16), vmem((parts, piece, piece), BF16),
            vmem((rows, width), F32), vmem((rows, width), BF16), vmem((rows, width), BF16),
            vmem((tiles, 2, 2, depth, own, width), F32),
            vmem((tiles, 2, depth, own, width), F32),
            vmem((tiles, depth, own, width), F32),
            vmem((tiles, depth, own, width), F32),
            vmem((tiles, depth, own, width), F32),
            dma((3,)), dma((parts,)), dma((tiles,)),
            dma((tiles,)), dma((tiles,)), dma((tiles,)), dma((tiles,)),
            dma((tiles, depth)), dma((tiles, depth)), dma((tiles, depth)), dma((tiles, depth)),
        ],
        compiler_params=pltpu.CompilerParams(
            collective_id=0, has_side_effects=True, vmem_limit_bytes=60 * 1024 * 1024),
        name="forward_scatter",
    )(l_panel, x_prior, b_rows, diag_blocks, coupling)


def solution(mesh):
    in_specs = (
        P("ens", "row"),
        P("row", "ens"),
        P("row", "ens"),
        P("ens", None, None),
        P("ens", None),
    )
    out_specs = P("row", "ens")
    return jax.shard_map(functools.partial(shards, mesh.shape["row"]), mesh=mesh,
                         in_specs=in_specs, out_specs=out_specs, check_vma=False)
```

```python
import functools

import jax
import jax.numpy as jnp
from jax import lax
from jax.experimental import pallas as pl
from jax.experimental.pallas import tpu as pltpu
from jax.sharding import PartitionSpec as P

MESH = pl.DeviceIdType.MESH
F32, BF16 = jnp.float32, jnp.bfloat16


def split(value):
    high = value.astype(BF16)
    return high, (value - high.astype(F32)).astype(BF16)


def mm(a, b):
    return jnp.dot(a, b, preferred_element_type=F32)


def dot3(a, b):
    return mm(a[0], b[0]) + mm(a[0], b[1]) + mm(a[1], b[0])


def inverses(blocks):
    size = blocks[0].shape[0]
    rows = lax.broadcasted_iota(jnp.int32, (size, size), 0)
    cols = lax.broadcasted_iota(jnp.int32, (size, size), 1)
    on_diag = rows == cols
    eye = jnp.where(on_diag, 1.0, 0.0)
    scaled, col_scale = [], []
    for block in blocks:
        diag = jnp.where(on_diag, block, 0.0)
        scaled.append(block / jnp.sum(diag, axis=1, keepdims=True))
        col_scale.append(1.0 / jnp.sum(diag, axis=0, keepdims=True))
    step = 8
    near = (rows > cols) & (rows // step == cols // step)
    low = [jnp.where(near, s, 0.0) for s in scaled]
    ls = [split(v) for v in low]
    sq = [dot3(v, v) for v in ls]
    sqs = [split(v) for v in sq]
    quad = [dot3(v, v) for v in sqs]
    inv = [eye - v for v in low]
    inv = [v + dot3(split(v), w) for v, w in zip(inv, sqs)]
    inv = [v + dot3(split(v), split(w)) for v, w in zip(inv, quad)]
    while step < size:
        wide = 2 * step
        below = (rows // wide == cols // wide) & (rows // step > cols // step)
        invs = [split(v) for v in inv]
        prod = [dot3(split(jnp.where(below, s, 0.0)), v) for s, v in zip(scaled, invs)]
        inv = [v - dot3(w, split(p)) for v, w, p in zip(inv, invs, prod)]
        step = wide
    return [v * c for v, c in zip(inv, col_scale)]


def kernel(n, l_hbm, x_hbm, b_hbm, d_hbm, c_hbm, out_ref,
           l32, x32, b32, d32, c32, lhi, llo, xhi, xlo, fhi, flo, ihi, ilo, pbuf,
           sbuf, prcv, yrcv, urcv, drcv,
           in_sem, l_sem, x_sem, psend, precv, ysend, yrecv, usend, urecv, dsend, drecv):
    me = lax.axis_index("row")
    core, y, z = me % 2, (me // 2) % 2, me // 4
    depth = n // 4
    tiles, _, _, _, own, width = sbuf.shape
    rows = l32.shape[0]
    half = d32.shape[1]
    piece = ihi.shape[1]
    parts = rows // piece
    partner = me + 1 - 2 * core
    across = me + 2 - 4 * y
    up, down = me + 4, me - 4

    def send(src, dst, ssem, rsem, target):
        return pltpu.make_async_remote_copy(
            src_ref=src, dst_ref=dst, send_sem=ssem, recv_sem=rsem,
            device_id={"row": target}, device_id_type=MESH)

    def local(src, dst, sem):
        return pltpu.make_async_copy(src, dst, sem)

    in_copies = [local(d_hbm, d32, in_sem.at[0]), local(c_hbm, c32, in_sem.at[1]),
                 local(b_hbm, b32, in_sem.at[2])]
    l_copies = [local(l_hbm.at[pl.ds(k * piece, piece)], l32.at[pl.ds(k * piece, piece)], l_sem.at[k])
                for k in range(parts)]

    def x_copy(t):
        cols = pl.ds(pl.multiple_of(t * width, width), width)
        return local(x_hbm.at[:, cols], x32.at[t], x_sem.at[t])

    in_copies[0].start()
    x_copy(0).start()
    for copy in l_copies:
        copy.start()
    in_copies[1].start()
    in_copies[2].start()
    for t in range(1, tiles):
        x_copy(t).start()

    barrier = pltpu.get_barrier_semaphore()

    def greet(target):
        pl.semaphore_signal(barrier, inc=1, device_id={"row": target}, device_id_type=MESH)

    greet(partner)
    greet(across)

    @pl.when(z > 0)
    def _():
        greet(down)

    @pl.when(z < depth - 1)
    def _():
        greet(up)

    in_copies[0].wait()
    blocks = []
    for k in range(parts):
        which, at = (k * piece) // half, (k * piece) % half
        blocks.append(d32[which, at:at + piece, at:at + piece])
    for k, inv in enumerate(inverses(blocks)):
        ihi[k], ilo[k] = split(inv)
    for which in range(2):
        r = slice(which * half, (which + 1) * half)
        fhi[r, r], flo[r, r] = split(d32[which])
    in_copies[1].wait()
    fhi[half:, :half], flo[half:, :half] = split(c32[...])
    for k in range(parts):
        l_copies[k].wait()
        r = slice(k * piece, (k + 1) * piece)
        lhi[r], llo[r] = split(l32[r])
    in_copies[2].wait()

    inside = (z > 0).astype(jnp.int32) + (z < depth - 1).astype(jnp.int32)
    pl.semaphore_wait(barrier, 2 + inside)

    def pair_copy(t):
        return send(sbuf.at[t, 1 - core], prcv.at[t], psend.at[t], precv.at[t], partner)

    def y_copy(t):
        return send(sbuf.at[t, core, 1 - y], yrcv.at[t], ysend.at[t], yrecv.at[t], across)

    def up_copy(t, o):
        return send(sbuf.at[t, core, y, o], urcv.at[t, o], usend.at[t, o], urecv.at[t, o], up)

    def down_copy(t, o):
        return send(sbuf.at[t, core, y, o], drcv.at[t, o], dsend.at[t, o], drecv.at[t, o], down)

    def stage_y(t):
        pair_copy(t).wait_recv()
        sbuf[t, core, 1 - y] += prcv[t, 1 - y]
        y_copy(t).start()
        sbuf[t, core, y] += prcv[t, y]

    def stage_z(t):
        y_copy(t).wait_recv()
        sbuf[t, core, y] += yrcv[t]

        @pl.when(z == 0)
        def _():
            for o in range(depth - 1, 0, -1):
                up_copy(t, o).start()

        @pl.when(z == depth - 1)
        def _():
            for o in range(depth - 1):
                down_copy(t, o).start()

    def ups(t):
        for o in range(depth - 1, 1, -1):
            @pl.when((z > 0) & (z < o))
            def _():
                up_copy(t, o).wait_recv()
                sbuf[t, core, y, o] += urcv[t, o]
                up_copy(t, o).start()

    def downs(t):
        for o in range(depth - 2):
            @pl.when((z < depth - 1) & (z > o))
            def _():
                down_copy(t, o).wait_recv()
                sbuf[t, core, y, o] += drcv[t, o]
                down_copy(t, o).start()

    lower = z < depth // 2

    def near(t):
        @pl.when(lower)
        def _():
            ups(t)

        @pl.when(jnp.logical_not(lower))
        def _():
            downs(t)

    def final(t):
        @pl.when(lower)
        def _():
            downs(t)

        @pl.when(jnp.logical_not(lower))
        def _():
            ups(t)

        @pl.when(z > 0)
        def _():
            up_copy(t, z).wait_recv()
            sbuf[t, core, y, z] += urcv[t, z]

        @pl.when(z < depth - 1)
        def _():
            down_copy(t, z).wait_recv()
            sbuf[t, core, y, z] += drcv[t, z]

        cols = pl.ds(pl.multiple_of(t * width, width), width)
        out_ref[:, cols] = -sbuf[t, core, y, z]

    def product(first, last):
        def step(k, carry):
            r = pl.ds(pl.multiple_of(k * piece, piece), piece)
            pbuf[r, :] = dot3((lhi[r, :], llo[r, :]), (xhi[...], xlo[...]))
            return carry
        lax.fori_loop(first, last, step, 0)

    def tile(t, carry):
        x_copy(t).wait()
        xhi[...], xlo[...] = split(x32[t])
        product(0, parts // 2)

        @pl.when(t >= 1)
        def _():
            stage_y(t - 1)

        product(parts // 2, parts)

        @pl.when(t >= 2)
        def _():
            stage_z(t - 2)

        @pl.when(t >= 3)
        def _():
            final(t - 3)

        mine = pl.ds(pl.multiple_of(me * own, own), own)
        cols = pl.ds(pl.multiple_of(t * width, width), width)
        pbuf[mine, :] -= b32[:, cols]
        solved = []
        for k in range(parts):
            r = slice(k * piece, (k + 1) * piece)
            rest = pbuf[r, :]
            for j, known in enumerate(solved):
                done = slice(j * piece, (j + 1) * piece)
                rest = rest - dot3((fhi[r, done], flo[r, done]), known)
            value = dot3((ihi[k], ilo[k]), split(rest))
            solved.append(split(value))
            for p in range(piece // own):
                g = k * (piece // own) + p
                sbuf[t, g % 2, (g // 2) % 2, g // 4] = value[p * own:(p + 1) * own]
        pair_copy(t).start()

        @pl.when(t >= 2)
        def _():
            near(t - 2)

        return carry

    lax.fori_loop(0, tiles, tile, 0)
    stage_y(tiles - 1)
    if tiles > 1:
        stage_z(tiles - 2)
    if tiles > 2:
        final(tiles - 3)
    if tiles > 1:
        near(tiles - 2)
    stage_z(tiles - 1)
    if tiles > 1:
        final(tiles - 2)
    near(tiles - 1)
    final(tiles - 1)

    def finish(t, carry):
        pair_copy(t).wait_send()
        y_copy(t).wait_send()
        for o in range(depth):
            @pl.when(z < o)
            def _():
                up_copy(t, o).wait_send()

            @pl.when(z > o)
            def _():
                down_copy(t, o).wait_send()
        return carry

    lax.fori_loop(0, tiles, finish, 0)


def shards(n, l_panel, x_prior, b_rows, diag_blocks, coupling):
    rows, inner = l_panel.shape
    nrhs = x_prior.shape[1]
    own = b_rows.shape[0]
    half = diag_blocks.shape[1]
    width = min(nrhs, 256)
    piece = min(half, 256)
    tiles, depth, parts = nrhs // width, n // 4, rows // piece
    dma = pltpu.SemaphoreType.DMA
    vmem = pltpu.VMEM
    any_spec = pl.BlockSpec(memory_space=pl.ANY)
    return pl.pallas_call(
        functools.partial(kernel, n),
        out_shape=jax.ShapeDtypeStruct((own, nrhs), F32),
        in_specs=[any_spec] * 5,
        out_specs=pl.BlockSpec(memory_space=pltpu.VMEM),
        scratch_shapes=[
            vmem((rows, inner), F32), vmem((tiles, inner, width), F32), vmem((own, nrhs), F32),
            vmem(diag_blocks.shape, F32), vmem(coupling.shape, F32),
            vmem((rows, inner), BF16), vmem((rows, inner), BF16),
            vmem((inner, width), BF16), vmem((inner, width), BF16),
            vmem((rows, rows), BF16), vmem((rows, rows), BF16),
            vmem((parts, piece, piece), BF16), vmem((parts, piece, piece), BF16),
            vmem((rows, width), F32),
            vmem((tiles, 2, 2, depth, own, width), F32),
            vmem((tiles, 2, depth, own, width), F32),
            vmem((tiles, depth, own, width), F32),
            vmem((tiles, depth, own, width), F32),
            vmem((tiles, depth, own, width), F32),
            dma((3,)), dma((parts,)), dma((tiles,)),
            dma((tiles,)), dma((tiles,)), dma((tiles,)), dma((tiles,)),
            dma((tiles, depth)), dma((tiles, depth)), dma((tiles, depth)), dma((tiles, depth)),
        ],
        compiler_params=pltpu.CompilerParams(
            collective_id=0, has_side_effects=True, vmem_limit_bytes=60 * 1024 * 1024),
        name="forward_scatter",
    )(l_panel, x_prior, b_rows, diag_blocks, coupling)


def solution(mesh):
    in_specs = (
        P("ens", "row"),
        P("row", "ens"),
        P("row", "ens"),
        P("ens", None, None),
        P("ens", None),
    )
    out_specs = P("row", "ens")
    return jax.shard_map(functools.partial(shards, mesh.shape["row"]), mesh=mesh,
                         in_specs=in_specs, out_specs=out_specs, check_vma=False)
```

```python
import functools

import jax
import jax.numpy as jnp
from jax import lax
from jax.experimental import pallas as pl
from jax.experimental.pallas import tpu as pltpu
from jax.sharding import PartitionSpec as P

MESH = pl.DeviceIdType.MESH
F32, BF16 = jnp.float32, jnp.bfloat16


def split(value):
    high = value.astype(BF16)
    return high, (value - high.astype(F32)).astype(BF16)


def mm(a, b):
    return jnp.dot(a, b, preferred_element_type=F32)


def dot3(a, b):
    return mm(a[0], b[0]) + mm(a[0], b[1]) + mm(a[1], b[0])


def inverses(blocks):
    size = blocks[0].shape[0]
    rows = lax.broadcasted_iota(jnp.int32, (size, size), 0)
    cols = lax.broadcasted_iota(jnp.int32, (size, size), 1)
    on_diag = rows == cols
    eye = jnp.where(on_diag, 1.0, 0.0)
    scaled, col_scale = [], []
    for block in blocks:
        diag = jnp.where(on_diag, block, 0.0)
        scaled.append(block / jnp.sum(diag, axis=1, keepdims=True))
        col_scale.append(1.0 / jnp.sum(diag, axis=0, keepdims=True))
    step = 8
    near = (rows > cols) & (rows // step == cols // step)
    low = [jnp.where(near, s, 0.0) for s in scaled]
    ls = [split(v) for v in low]
    sq = [dot3(v, v) for v in ls]
    sqs = [split(v) for v in sq]
    quad = [dot3(v, v) for v in sqs]
    inv = [eye - v for v in low]
    inv = [v + dot3(split(v), w) for v, w in zip(inv, sqs)]
    inv = [v + dot3(split(v), split(w)) for v, w in zip(inv, quad)]
    while step < size:
        wide = 2 * step
        below = (rows // wide == cols // wide) & (rows // step > cols // step)
        invs = [split(v) for v in inv]
        prod = [dot3(split(jnp.where(below, s, 0.0)), v) for s, v in zip(scaled, invs)]
        inv = [v - dot3(w, split(p)) for v, w, p in zip(inv, invs, prod)]
        step = wide
    return [v * c for v, c in zip(inv, col_scale)]


def kernel(n, l_hbm, x_hbm, b_hbm, d_hbm, c_hbm, out_ref,
           l32, x32, b32, d32, c32, lhi, llo, xhi, xlo, fhi, flo, ihi, ilo, pbuf,
           sbuf, prcv, yrcv, urcv, drcv,
           in_sem, l_sem, x_sem, psend, precv, ysend, yrecv, usend, urecv, dsend, drecv):
    me = lax.axis_index("row")
    core, y, z = me % 2, (me // 2) % 2, me // 4
    depth = n // 4
    tiles, _, _, _, own, width = sbuf.shape
    rows = l32.shape[0]
    half = d32.shape[1]
    piece = ihi.shape[1]
    parts = rows // piece
    partner = me + 1 - 2 * core
    across = me + 2 - 4 * y
    up, down = me + 4, me - 4

    def send(src, dst, ssem, rsem, target):
        return pltpu.make_async_remote_copy(
            src_ref=src, dst_ref=dst, send_sem=ssem, recv_sem=rsem,
            device_id={"row": target}, device_id_type=MESH)

    def local(src, dst, sem):
        return pltpu.make_async_copy(src, dst, sem)

    in_copies = [local(d_hbm, d32, in_sem.at[0]), local(c_hbm, c32, in_sem.at[1]),
                 local(b_hbm, b32, in_sem.at[2])]
    l_copies = [local(l_hbm.at[pl.ds(k * piece, piece)], l32.at[pl.ds(k * piece, piece)], l_sem.at[k])
                for k in range(parts)]

    def x_copy(t):
        cols = pl.ds(pl.multiple_of(t * width, width), width)
        return local(x_hbm.at[:, cols], x32.at[t], x_sem.at[t])

    in_copies[0].start()
    x_copy(0).start()
    for copy in l_copies:
        copy.start()
    in_copies[1].start()
    in_copies[2].start()
    for t in range(1, tiles):
        x_copy(t).start()

    barrier = pltpu.get_barrier_semaphore()

    def greet(target):
        pl.semaphore_signal(barrier, inc=1, device_id={"row": target}, device_id_type=MESH)

    greet(partner)
    greet(across)

    @pl.when(z > 0)
    def _():
        greet(down)

    @pl.when(z < depth - 1)
    def _():
        greet(up)

    in_copies[0].wait()
    blocks = []
    for k in range(parts):
        which, at = (k * piece) // half, (k * piece) % half
        blocks.append(d32[which, at:at + piece, at:at + piece])
    for k, inv in enumerate(inverses(blocks)):
        ihi[k], ilo[k] = split(inv)
    for which in range(2):
        r = slice(which * half, (which + 1) * half)
        fhi[r, r], flo[r, r] = split(d32[which])
    in_copies[1].wait()
    fhi[half:, :half], flo[half:, :half] = split(c32[...])
    for k in range(parts):
        l_copies[k].wait()
        r = slice(k * piece, (k + 1) * piece)
        lhi[r], llo[r] = split(l32[r])
    in_copies[2].wait()

    inside = (z > 0).astype(jnp.int32) + (z < depth - 1).astype(jnp.int32)
    pl.semaphore_wait(barrier, 2 + inside)

    def pair_copy(t):
        return send(sbuf.at[t, 1 - core], prcv.at[t], psend.at[t], precv.at[t], partner)

    def y_copy(t):
        return send(sbuf.at[t, core, 1 - y], yrcv.at[t], ysend.at[t], yrecv.at[t], across)

    def up_copy(t, o):
        return send(sbuf.at[t, core, y, o], urcv.at[t, o], usend.at[t, o], urecv.at[t, o], up)

    def down_copy(t, o):
        return send(sbuf.at[t, core, y, o], drcv.at[t, o], dsend.at[t, o], drecv.at[t, o], down)

    def stage_y(t):
        pair_copy(t).wait_recv()
        sbuf[t, core, 1 - y] += prcv[t, 1 - y]
        y_copy(t).start()
        sbuf[t, core, y] += prcv[t, y]

    def stage_z(t):
        y_copy(t).wait_recv()
        for o in range(depth - 1, 0, -1):
            sbuf[t, core, y, o] += yrcv[t, o]

            @pl.when(z == 0)
            def _():
                up_copy(t, o).start()

        sbuf[t, core, y, 0] += yrcv[t, 0]

        @pl.when(z == depth - 1)
        def _():
            for o in range(depth - 1):
                down_copy(t, o).start()

    def ups(t):
        for o in range(depth - 1, 1, -1):
            @pl.when((z > 0) & (z < o))
            def _():
                up_copy(t, o).wait_recv()
                sbuf[t, core, y, o] += urcv[t, o]
                up_copy(t, o).start()

    def downs(t):
        for o in range(depth - 2):
            @pl.when((z < depth - 1) & (z > o))
            def _():
                down_copy(t, o).wait_recv()
                sbuf[t, core, y, o] += drcv[t, o]
                down_copy(t, o).start()

    lower = z < depth // 2

    def near(t):
        @pl.when(lower)
        def _():
            ups(t)

        @pl.when(jnp.logical_not(lower))
        def _():
            downs(t)

    def final(t):
        @pl.when(lower)
        def _():
            downs(t)

        @pl.when(jnp.logical_not(lower))
        def _():
            ups(t)

        @pl.when(z > 0)
        def _():
            up_copy(t, z).wait_recv()
            sbuf[t, core, y, z] += urcv[t, z]

        @pl.when(z < depth - 1)
        def _():
            down_copy(t, z).wait_recv()
            sbuf[t, core, y, z] += drcv[t, z]

        cols = pl.ds(pl.multiple_of(t * width, width), width)
        out_ref[:, cols] = -sbuf[t, core, y, z]

    def product(first, last):
        def step(k, carry):
            r = pl.ds(pl.multiple_of(k * piece, piece), piece)
            pbuf[r, :] = dot3((lhi[r, :], llo[r, :]), (xhi[...], xlo[...]))
            return carry
        lax.fori_loop(first, last, step, 0)

    def tile(t, carry):
        x_copy(t).wait()
        xhi[...], xlo[...] = split(x32[t])
        product(0, parts // 2)

        @pl.when(t >= 1)
        def _():
            stage_y(t - 1)

        product(parts // 2, parts)

        @pl.when(t >= 2)
        def _():
            stage_z(t - 2)

        mine = pl.ds(pl.multiple_of(me * own, own), own)
        cols = pl.ds(pl.multiple_of(t * width, width), width)
        pbuf[mine, :] -= b32[:, cols]
        solved = []
        for k in range(parts):
            r = slice(k * piece, (k + 1) * piece)
            rest = pbuf[r, :]
            for j, known in enumerate(solved):
                done = slice(j * piece, (j + 1) * piece)
                rest = rest - dot3((fhi[r, done], flo[r, done]), known)
            value = dot3((ihi[k], ilo[k]), split(rest))
            solved.append(split(value))
            for p in range(piece // own):
                g = k * (piece // own) + p
                sbuf[t, g % 2, (g // 2) % 2, g // 4] = value[p * own:(p + 1) * own]
        pair_copy(t).start()

        @pl.when(t >= 3)
        def _():
            final(t - 3)

        @pl.when(t >= 2)
        def _():
            near(t - 2)

        return carry

    lax.fori_loop(0, tiles, tile, 0)
    stage_y(tiles - 1)
    if tiles > 1:
        stage_z(tiles - 2)
    if tiles > 2:
        final(tiles - 3)
    if tiles > 1:
        near(tiles - 2)
    stage_z(tiles - 1)
    if tiles > 1:
        final(tiles - 2)
    near(tiles - 1)
    final(tiles - 1)

    def finish(t, carry):
        pair_copy(t).wait_send()
        y_copy(t).wait_send()
        for o in range(depth):
            @pl.when(z < o)
            def _():
                up_copy(t, o).wait_send()

            @pl.when(z > o)
            def _():
                down_copy(t, o).wait_send()
        return carry

    lax.fori_loop(0, tiles, finish, 0)


def shards(n, l_panel, x_prior, b_rows, diag_blocks, coupling):
    rows, inner = l_panel.shape
    nrhs = x_prior.shape[1]
    own = b_rows.shape[0]
    half = diag_blocks.shape[1]
    width = min(nrhs, 256)
    piece = min(half, 256)
    tiles, depth, parts = nrhs // width, n // 4, rows // piece
    dma = pltpu.SemaphoreType.DMA
    vmem = pltpu.VMEM
    any_spec = pl.BlockSpec(memory_space=pl.ANY)
    return pl.pallas_call(
        functools.partial(kernel, n),
        out_shape=jax.ShapeDtypeStruct((own, nrhs), F32),
        in_specs=[any_spec] * 5,
        out_specs=pl.BlockSpec(memory_space=pltpu.VMEM),
        scratch_shapes=[
            vmem((rows, inner), F32), vmem((tiles, inner, width), F32), vmem((own, nrhs), F32),
            vmem(diag_blocks.shape, F32), vmem(coupling.shape, F32),
            vmem((rows, inner), BF16), vmem((rows, inner), BF16),
            vmem((inner, width), BF16), vmem((inner, width), BF16),
            vmem((rows, rows), BF16), vmem((rows, rows), BF16),
            vmem((parts, piece, piece), BF16), vmem((parts, piece, piece), BF16),
            vmem((rows, width), F32),
            vmem((tiles, 2, 2, depth, own, width), F32),
            vmem((tiles, 2, depth, own, width), F32),
            vmem((tiles, depth, own, width), F32),
            vmem((tiles, depth, own, width), F32),
            vmem((tiles, depth, own, width), F32),
            dma((3,)), dma((parts,)), dma((tiles,)),
            dma((tiles,)), dma((tiles,)), dma((tiles,)), dma((tiles,)),
            dma((tiles, depth)), dma((tiles, depth)), dma((tiles, depth)), dma((tiles, depth)),
        ],
        compiler_params=pltpu.CompilerParams(
            collective_id=0, has_side_effects=True, vmem_limit_bytes=60 * 1024 * 1024),
        name="forward_scatter",
    )(l_panel, x_prior, b_rows, diag_blocks, coupling)


def solution(mesh):
    in_specs = (
        P("ens", "row"),
        P("row", "ens"),
        P("row", "ens"),
        P("ens", None, None),
        P("ens", None),
    )
    out_specs = P("row", "ens")
    return jax.shard_map(functools.partial(shards, mesh.shape["row"]), mesh=mesh,
                         in_specs=in_specs, out_specs=out_specs, check_vma=False)
```
